512 devices in a mesh: layer: 16 (over x_hi, z), row: 8 (over y), col: 4 (over x_lo, core).
Axes of the slice: x: 4 (x_hi: 2, x_lo: 2; x = x_hi * 2 + x_lo), y: 8, z: 8, core: 2. Of those that a mesh axis runs over, the one named last changes fastest.
Arguments:
- sources: bfloat16 [16, 64, 16, 16, 128], P('layer', None, 'row', 'col'), may hold values from -3 to 3
- adjoint_sources: bfloat16 [16, 64, 16, 16, 128], P('layer', None, 'row', 'col'), may hold values from -3 to 3
- blocks: bfloat16 [16, 16, 16, 9, 128, 128], P('layer', 'row', 'col'), may hold values from -0.2 to 1.4
- pattern: int32 [16, 16, 16, 9], P('layer', 'row', 'col'), may hold values 0 or 1
- coupling: float32 [4], replicated, may hold values from 0.7 to 0.9
- layer_group: int32 [16], replicated, may hold values from 0 to 3
- port_cells: int32 [64], replicated, may hold values from 0 to 32767
Outputs:
- forward_field: bfloat16 [16, 64, 16, 16, 128], P('layer', None, 'row', 'col')
- adjoint_field: bfloat16 [16, 64, 16, 16, 128], P('layer', None, 'row', 'col')
- gradient: float32 [4, 16, 16, 128], P(None, 'row', 'col')
The draws below stay inside these ranges and needn't reach their ends.
All inputs are finite; a program needn't handle non-finite values. No bound on the sum of `pattern` on one device may be relied on, other than what follows from the above.
Results may differ from the reference program's by a relative error of at most 0.01.
Values may be sent and summed in bfloat16 or wider, within the bound.
A program may use at most 64 MiB of HBM per device.

```python
import math
import jax
import jax.numpy as jnp
from jax import lax

TILE = 128
PORTS = 64
NG = 4
L = 16
NTX = 16
NTY = 16
F = 32768


def draw_blocks(key, part):
    full_shape = (L, NTX, NTY, 9, TILE, TILE)
    spread = 0.3 / math.sqrt(6.0 * TILE)
    random_part = jax.random.normal(key, full_shape, jnp.float32) * spread
    center = (jnp.arange(9) == 4).astype(jnp.float32)[:, None, None] * jnp.eye(TILE, dtype=jnp.float32)[None] * 1.25
    return (random_part + center[None, None, None]).astype(jnp.bfloat16)


def touch_ends(entries, key, least, top_value):
    longest = entries.shape.index(max(entries.shape))
    spots = []
    for shift in (0, 1):
        where = [jax.random.randint(jax.random.fold_in(key, axis), (), 0, length) for axis, length in enumerate(entries.shape)]
        where[longest] = (where[longest] + shift) % entries.shape[longest]
        spots.append(tuple(where))
    return entries.at[spots[0]].set(least).at[spots[1]].set(top_value)


def block_levels(stream_key, shape, split, least, largest):
    loudness, own = 1.0, jax.random.fold_in(stream_key, 6)
    for dim, shards_of in split:
        heights = jnp.exp(jax.random.uniform(jax.random.fold_in(own, dim), (shards_of,), jnp.float32, least / len(split), largest / len(split)))
        loudness = loudness * jnp.repeat(heights, shape[dim] // shards_of).reshape([-1 if axis == dim else 1 for axis in range(len(shape))])
    return loudness


def normal_values(own_key, shape, deviation, most, split=(), kind=jnp.bfloat16):
    entries = jax.random.normal(own_key, shape, jnp.float32) * deviation
    if len(split) > 0:
        entries = block_levels(own_key, shape, split, -0.22, 0.18) * entries
    return jnp.clip(entries, min=-most, max=most).astype(kind)


def setup_inputs(seed: int = 0) -> dict:
    seeds = jax.random.split(jax.random.key(seed), 8)
    sources = normal_values(seeds[0], (L, PORTS, NTX, NTY, TILE), 0.5, 3.0, ((0, 16), (2, 8), (3, 4)))
    adjoint_sources = normal_values(seeds[1], (L, PORTS, NTX, NTY, TILE), 0.5, 3.0, ((0, 16), (2, 8), (3, 4)))
    blocks = draw_blocks(jax.random.fold_in(seeds[7], 71), 0)
    pattern = touch_ends((jax.random.randint(seeds[3], (L, NTX, NTY, 9), 0, 3) < 2).astype(jnp.int32), jax.random.fold_in(seeds[3], 1), 0, 1)
    coupling = jnp.clip(jax.random.uniform(seeds[4], (NG,), jnp.float32, 0.7, 0.9), 0.7, 0.9)
    layer_group = touch_ends(jax.random.randint(seeds[5], (L,), 0, NG), jax.random.fold_in(seeds[5], 1), 0, NG - 1).astype(jnp.int32)
    port_cells = touch_ends(jax.random.randint(seeds[6], (PORTS,), 0, F), jax.random.fold_in(seeds[6], 1), 0, F - 1).astype(jnp.int32)
    return {"sources": sources, "adjoint_sources": adjoint_sources, "blocks": blocks, "pattern": pattern, "coupling": coupling, "layer_group": layer_group, "port_cells": port_cells}


port_strength = 4.0
intersection_scale = 0.125


def apply_front(wave, front_blocks, front_mask):
    padded = jnp.pad(wave.astype(jnp.float32), ((0, 0), (1, 1), (1, 1), (0, 0)))
    summed = jnp.zeros(wave.shape, jnp.float32)
    for offset in range(9):
        step_x = offset // 3 - 1
        step_y = offset % 3 - 1
        beside = padded[:, 1 + step_x:1 + step_x + NTX, 1 + step_y:1 + step_y + NTY, :]
        product_term = jnp.einsum("pijc,ijcd->pijd", beside, front_blocks[:, :, offset].astype(jnp.float32), precision=lax.Precision.HIGHEST)
        summed = summed + front_mask[None, :, :, offset, None].astype(jnp.float32) * product_term
    return summed


def reference(sources, adjoint_sources, blocks, pattern, coupling, layer_group, port_cells):
    member = (layer_group[:, None] == jnp.arange(NG, dtype=jnp.int32)[None, :]).astype(jnp.float32)
    kappa = jnp.dot(member, coupling, precision=lax.Precision.HIGHEST)
    kappa_next = jnp.concatenate([kappa[1:], jnp.zeros((1,), jnp.float32)])
    cell_ids = jnp.arange(NTX * NTY * TILE, dtype=jnp.int32).reshape(NTX, NTY, TILE)
    port_map = (cell_ids[None] == port_cells[:, None, None, None]).astype(jnp.float32) * port_strength
    layer_ids = jnp.arange(L, dtype=jnp.int32)
    first_flag = (layer_ids == 0).astype(jnp.float32)
    last_flag = (layer_ids == L - 1).astype(jnp.float32)

    def sweep_step(previous, inputs):
        source_layer, front_blocks, front_mask, strength, flag_value = inputs
        wave = (source_layer.astype(jnp.float32) + flag_value * port_map + strength * previous.astype(jnp.float32)).astype(jnp.bfloat16)
        result = apply_front(wave, front_blocks, front_mask).astype(jnp.bfloat16)
        return result, result

    empty = jnp.zeros((PORTS, NTX, NTY, TILE), jnp.bfloat16)
    _, forward_field = lax.scan(sweep_step, empty, (sources, blocks, pattern, kappa, first_flag))
    _, adjoint_field = lax.scan(sweep_step, empty, (adjoint_sources, blocks, pattern, kappa_next, last_flag), reverse=True)
    intersection = jnp.sum(forward_field.astype(jnp.float32) * adjoint_field.astype(jnp.float32), axis=1) * intersection_scale
    gradient = jnp.einsum("lg,lxyc->gxyc", member, intersection, precision=lax.Precision.HIGHEST)
    return forward_field, adjoint_field, gradient
```

```python
import functools

import jax
import jax.numpy as jnp
from jax import lax
from jax.experimental import pallas as pl
from jax.experimental.pallas import tpu as pltpu
from jax.sharding import PartitionSpec as P

port_strength = 4.0
intersection_scale = 0.125

LAYERS, ROWS, COLS = 16, 8, 4
TX, TY = 2, 4
PORTS, TILE, GROUPS = 64, 128, 4
CHUNK = 16
CHUNKS = PORTS // CHUNK
MESH = pl.DeviceIdType.MESH

BESIDE = [(-1, -1), (-1, 1), (1, -1), (1, 1), (-1, 0), (1, 0), (0, -1), (0, 1), (0, 0)]
MINE_X = {-1: pl.ds(0, 1), 0: pl.ds(0, 2), 1: pl.ds(1, 1)}
MINE_Y = {-1: pl.ds(0, 1), 0: pl.ds(0, 4), 1: pl.ds(3, 1)}
THERE_X = {-1: pl.ds(3, 1), 0: pl.ds(1, 2), 1: pl.ds(0, 1)}
THERE_Y = {-1: pl.ds(5, 1), 0: pl.ds(1, 4), 1: pl.ds(0, 1)}


def kernel(
    forward_rhs,
    adjoint_rhs,
    blocks,
    pattern,
    coupling,
    layer_group,
    fields,
    gradient,
    weights,
    framed,
    waves,
    coming,
    partial,
    mine,
    theirs,
    load_sem,
    send_sem,
    recv_sem,
    start_send,
    ahead_send,
    ahead_recv,
    sum_send,
    sum_recv,
):
    layer, row, col = (lax.axis_index(a) for a in ("layer", "row", "col"))
    first_layer, last_layer = layer == 0, layer == LAYERS - 1

    loading = pltpu.make_async_copy(blocks, weights, load_sem)
    loading.start()

    def beside(a, b):
        ok = None
        for cond in (
            [row > 0] if a < 0 else [row < ROWS - 1] if a > 0 else []
        ) + ([col > 0] if b < 0 else [col < COLS - 1] if b > 0 else []):
            ok = cond if ok is None else jnp.logical_and(ok, cond)
        return ok

    def when(*conds):
        conds = [c for c in conds if c is not None]
        return pl.when(functools.reduce(jnp.logical_and, conds)) if conds else (lambda f: f())

    def device(to_layer, a=0, b=0):
        return {"layer": to_layer, "row": row + a, "col": col + b}

    for edge, where in (
        (row == 0, (0, slice(None))),
        (row == ROWS - 1, (3, slice(None))),
        (col == 0, (slice(None), 0)),
        (col == COLS - 1, (slice(None), 5)),
    ):

        @pl.when(edge)
        def _(where=where):
            for s in range(2):
                for c in range(CHUNKS):
                    view = framed.at[(s, c) + where]
                    view[...] = jnp.zeros(view.shape, jnp.bfloat16)

    barrier = pltpu.get_barrier_semaphore()

    def greet(to_layer, a, b):
        pl.semaphore_signal(barrier, 1, device_id=device(to_layer, a, b), device_id_type=MESH)

    rows_beside = 3 - jnp.where(row == 0, 1, 0) - jnp.where(row == ROWS - 1, 1, 0)
    cols_beside = 3 - jnp.where(col == 0, 1, 0) - jnp.where(col == COLS - 1, 1, 0)
    edge_layer = jnp.where(jnp.logical_or(first_layer, last_layer), 1, 0)
    for a, b in BESIDE[:-1]:

        @when(beside(a, b), layer > 0)
        def _(a=a, b=b):
            greet(layer - 1, a, b)

        @when(beside(a, b), layer < LAYERS - 1)
        def _(a=a, b=b):
            greet(layer + 1, a, b)

        @when(beside(a, b), edge_layer == 1)
        def _(a=a, b=b):
            greet(layer, a, b)

    def greet_layer(k, _):
        greet(lax.rem(layer + k, LAYERS), 0, 0)
        return 0

    lax.fori_loop(1, LAYERS, greet_layer, 0)
    around = rows_beside * cols_beside - 1
    pl.semaphore_wait(barrier, LAYERS - 1 + around * 2)

    def ahead(s, c):
        return pltpu.make_async_remote_copy(
            src_ref=own(s, c),
            dst_ref=coming.at[s, :, :, pl.ds(c * CHUNK, CHUNK)],
            send_sem=ahead_send.at[s, c],
            recv_sem=ahead_recv.at[s, c],
            device_id=device(layer - 1 + 2 * s),
            device_id_type=MESH,
        )

    def hop(s, c, a, b, to_layer, source, sem):
        at = 3 * (a + 1) + b + 1
        return pltpu.make_async_remote_copy(
            src_ref=source.at[MINE_X[a], MINE_Y[b]],
            dst_ref=framed.at[s, c, THERE_X[a], THERE_Y[b]],
            send_sem=sem.at[c, at],
            recv_sem=recv_sem.at[s, c, at],
            device_id=device(to_layer, a, b),
            device_id_type=MESH,
        )

    def own(s, c):
        ports = pl.ds(pl.multiple_of(c * CHUNK, CHUNK), CHUNK)
        return (forward_rhs, adjoint_rhs)[s].at[:, :, ports]

    for s, starts in ((0, first_layer), (1, last_layer)):

        @pl.when(starts)
        def _(s=s):
            for c in range(CHUNKS):
                source = own(s, c)
                for a, b in BESIDE[:-1]:

                    @when(beside(a, b))
                    def _(a=a, b=b):
                        hop(s, c, a, b, layer, source, start_send).start()

                pltpu.make_async_copy(
                    source, framed.at[s, c, pl.ds(1, TX), pl.ds(1, TY)], recv_sem.at[s, c, 4]
                ).start()

    for s, sends in ((0, layer > 0), (1, layer < LAYERS - 1)):

        @pl.when(sends)
        def _(s=s):
            for c in range(CHUNKS):
                ahead(s, c).start()

    loading.wait()
    for i in range(TX):
        for j in range(TY):

            def mask(k, _, i=i, j=j):
                present = pattern[i, j, k].astype(jnp.float32).astype(jnp.bfloat16)
                weights[i, j, k] = weights[i, j, k] * present
                return 0

            lax.fori_loop(0, 9, mask, 0)

    partial[...] = jnp.zeros(partial.shape, jnp.float32)
    kappa_next = coupling[layer_group[jnp.minimum(layer + 1, LAYERS - 1)]]
    kappa_own = coupling[layer_group[layer]]

    late = jnp.where(layer < LAYERS // 2, 0, 1)

    def step(n, _):
        phase, c = n // CHUNKS, lax.rem(n, CHUNKS)
        s = lax.rem(phase + late, 2)
        to_layer = layer + 1 - 2 * s
        goes_on = jnp.where(s == 0, layer < LAYERS - 1, layer > 0)
        kappa = jnp.where(s == 0, kappa_next, kappa_own)
        ports = pl.ds(pl.multiple_of(c * CHUNK, CHUNK), CHUNK)

        @pl.when(goes_on)
        def _():
            pltpu.make_async_copy(
                coming.at[s, :, :, ports], coming.at[s, :, :, ports], ahead_recv.at[s, c]
            ).wait()

        for a, b in reversed(BESIDE):
            @when(beside(-a, -b))
            def _(a=a, b=b):
                landed = framed.at[s, c, THERE_X[a], THERE_Y[b]]
                pltpu.make_async_copy(
                    landed, landed, recv_sem.at[s, c, 3 * (a + 1) + b + 1]
                ).wait()

        for i in range(TX):
            for j in range(TY):
                lhs = jnp.concatenate(
                    [framed[s, c, i + k // 3, j + k % 3] for k in range(9)], axis=-1
                )
                rhs = weights[i, j].reshape(9 * TILE, TILE)
                field = jnp.dot(lhs, rhs, preferred_element_type=jnp.float32).astype(jnp.bfloat16)
                fields[s, i, j, ports] = field
                waves[s, c, i, j] = (
                    coming[s, i, j, ports].astype(jnp.float32) + kappa * field.astype(jnp.float32)
                ).astype(jnp.bfloat16)

        @pl.when(goes_on)
        def _():
            for a, b in BESIDE:

                @when(beside(a, b))
                def _(a=a, b=b):
                    hop(s, c, a, b, to_layer, waves.at[s, c], send_sem.at[s]).start()

        @pl.when(phase == 1)
        def _():
            for i in range(TX):
                for j in range(TY):
                    both = fields[0, i, j, ports].astype(jnp.float32) * fields[
                        1, i, j, ports
                    ].astype(jnp.float32)
                    partial[TY * i + j] += both

        return 0

    lax.fori_loop(0, 2 * CHUNKS, step, 0)

    for t in range(TX * TY):
        mine[pl.ds(t, 1)] = jnp.sum(partial[t], axis=0, keepdims=True) * intersection_scale

    def share(k):
        return pltpu.make_async_remote_copy(
            src_ref=mine,
            dst_ref=theirs.at[k],
            send_sem=sum_send.at[k],
            recv_sem=sum_recv.at[k],
            device_id=device(lax.rem(layer + k, LAYERS)),
            device_id_type=MESH,
        )

    def start_share(k, _):
        share(k).start()
        return 0

    lax.fori_loop(1, LAYERS, start_share, 0)
    theirs[0] = mine[...]

    for s, sends in ((0, layer > 0), (1, layer < LAYERS - 1)):

        @pl.when(sends)
        def _(s=s):
            for c in range(CHUNKS):
                ahead(s, c).wait_send()

    for s, starts, sends in ((0, first_layer, layer < LAYERS - 1), (1, last_layer, layer > 0)):

        def drain(c, _, s=s, sem=None):
            for a, b in BESIDE if sem is None else BESIDE[:-1]:

                @when(beside(a, b))
                def _(a=a, b=b):
                    out = send_sem.at[s] if sem is None else sem
                    hop(s, c, a, b, layer, waves.at[s, c], out).wait_send()

            return 0

        @pl.when(sends)
        def _(drain=drain):
            lax.fori_loop(0, CHUNKS, drain, 0)

        @pl.when(starts)
        def _(drain=drain):
            lax.fori_loop(0, CHUNKS, functools.partial(drain, sem=start_send), 0)

    def end_share(k, _):
        share(k).wait()
        return 0

    lax.fori_loop(1, LAYERS, end_share, 0)
    for g in range(GROUPS):

        def add(k, total, g=g):
            other = lax.rem(layer - k + LAYERS, LAYERS)
            chosen = jnp.where(layer_group[other] == g, 1.0, 0.0).astype(jnp.float32)
            return total + chosen * theirs[k]

        gradient[g] = lax.fori_loop(
            0, LAYERS, add, jnp.zeros((TX * TY, TILE), jnp.float32)
        )


def sweeps(forward_rhs, adjoint_rhs, blocks, pattern, coupling, layer_group):
    vmem, smem = (pl.BlockSpec(memory_space=m) for m in (pltpu.VMEM, pltpu.SMEM))
    return pl.pallas_call(
        kernel,
        out_shape=(
            jax.ShapeDtypeStruct((2, TX, TY, PORTS, TILE), jnp.bfloat16),
            jax.ShapeDtypeStruct((GROUPS, TX * TY, TILE), jnp.float32),
        ),
        in_specs=[vmem, vmem, pl.BlockSpec(memory_space=pl.ANY), smem, smem, smem],
        out_specs=(vmem, vmem),
        scratch_shapes=[
            pltpu.VMEM((TX, TY, 9, TILE, TILE), jnp.bfloat16),
            pltpu.VMEM((2, CHUNKS, TX + 2, TY + 2, CHUNK, TILE), jnp.bfloat16),
            pltpu.VMEM((2, CHUNKS, TX, TY, CHUNK, TILE), jnp.bfloat16),
            pltpu.VMEM((2, TX, TY, PORTS, TILE), jnp.bfloat16),
            pltpu.VMEM((TX * TY, CHUNK, TILE), jnp.float32),
            pltpu.VMEM((TX * TY, TILE), jnp.float32),
            pltpu.VMEM((LAYERS, TX * TY, TILE), jnp.float32),
            pltpu.SemaphoreType.DMA,
            pltpu.SemaphoreType.DMA((2, CHUNKS, 9)),
            pltpu.SemaphoreType.DMA((2, CHUNKS, 9)),
            pltpu.SemaphoreType.DMA((CHUNKS, 9)),
            pltpu.SemaphoreType.DMA((2, CHUNKS)),
            pltpu.SemaphoreType.DMA((2, CHUNKS)),
            pltpu.SemaphoreType.DMA((LAYERS,)),
            pltpu.SemaphoreType.DMA((LAYERS,)),
        ],
        compiler_params=pltpu.CompilerParams(
            collective_id=0, has_side_effects=True, vmem_limit_bytes=32 << 20
        ),
        name="sweeps",
    )(forward_rhs, adjoint_rhs, blocks, pattern, coupling, layer_group)


def local(sources, adjoint_sources, blocks, pattern, coupling, layer_group, port_cells):
    layer, row, col = (lax.axis_index(a) for a in ("layer", "row", "col"))
    x = row * TX + lax.broadcasted_iota(jnp.int32, (1, TX, TY, TILE), 1)
    y = col * TY + lax.broadcasted_iota(jnp.int32, (1, TX, TY, TILE), 2)
    cell = (x * (COLS * TY) + y) * TILE + lax.broadcasted_iota(jnp.int32, (1, TX, TY, TILE), 3)
    port_map = jnp.where(cell == port_cells[:, None, None, None], port_strength, 0.0)

    def rhs(array, flag):
        whole = array[0].astype(jnp.float32) + jnp.where(flag, 1.0, 0.0) * port_map
        return jnp.transpose(whole.astype(jnp.bfloat16), (1, 2, 0, 3))

    fields, gradient = sweeps(
        rhs(sources, layer == 0),
        rhs(adjoint_sources, layer == LAYERS - 1),
        blocks[0],
        pattern[0],
        coupling,
        layer_group,
    )
    fields = jnp.transpose(fields, (0, 3, 1, 2, 4))
    return (fields[:1], fields[1:], gradient.reshape(GROUPS, TX, TY, TILE))


def solution(mesh):
    placed = (
        P("layer", None, "row", "col", None),
        P("layer", None, "row", "col", None),
        P("layer", "row", "col", None, None, None),
        P("layer", "row", "col", None),
        P(),
        P(),
        P(),
    )
    return jax.shard_map(
        local,
        mesh=mesh,
        in_specs=placed,
        out_specs=(
            P("layer", None, "row", "col", None),
            P("layer", None, "row", "col", None),
            P(None, "row", "col", None),
        ),
        check_vma=False,
    )
```

```python
import functools

import jax
import jax.numpy as jnp
from jax import lax
from jax.experimental import pallas as pl
from jax.experimental.pallas import tpu as pltpu
from jax.sharding import PartitionSpec as P

port_strength = 4.0
intersection_scale = 0.125

LAYERS, ROWS, COLS = 16, 8, 4
TX, TY = 2, 4
PORTS, TILE, GROUPS = 64, 128, 4
CHUNK = 8
CHUNKS = PORTS // CHUNK
LAG = 4
MESH = pl.DeviceIdType.MESH

UP = [(-1, -1), (-1, 1), (-1, 0)]
DOWN = [(1, -1), (1, 1), (1, 0)]
LEVEL = [(0, -1), (0, 1)]
BESIDE = UP + DOWN + LEVEL
MINE_X = {-1: pl.ds(0, 1), 0: pl.ds(0, 2), 1: pl.ds(1, 1)}
MINE_Y = {-1: pl.ds(0, 1), 0: pl.ds(0, 4), 1: pl.ds(3, 1)}
THERE_X = {-1: pl.ds(3, 1), 0: pl.ds(1, 2), 1: pl.ds(0, 1)}
THERE_Y = {-1: pl.ds(5, 1), 0: pl.ds(1, 4), 1: pl.ds(0, 1)}
OWN, ABOVE, ASIDE = 0, 1, 2


def kernel(
    forward_rhs,
    adjoint_rhs,
    blocks,
    pattern,
    coupling,
    layer_group,
    forward_field,
    adjoint_field,
    gradient,
    weights,
    framed,
    waves,
    fields,
    coming,
    partial,
    mine,
    theirs,
    load_sem,
    send_sem,
    recv_sem,
    start_send,
    ahead_send,
    ahead_recv,
    sum_send,
    sum_recv,
):
    layer, row, col = (lax.axis_index(a) for a in ("layer", "row", "col"))
    first_layer, last_layer = layer == 0, layer == LAYERS - 1

    loading = pltpu.make_async_copy(blocks, weights, load_sem)
    loading.start()

    def beside(a, b):
        conds = [[row > 0], [], [row < ROWS - 1]][a + 1] + [[col > 0], [], [col < COLS - 1]][b + 1]
        return functools.reduce(jnp.logical_and, conds) if conds else None

    def when(*conds):
        conds = [c for c in conds if c is not None]
        return pl.when(functools.reduce(jnp.logical_and, conds)) if conds else (lambda f: f())

    def device(to_layer, a=0, b=0):
        return {"layer": to_layer, "row": row + a, "col": col + b}

    barrier = pltpu.get_barrier_semaphore()

    def greet(to_layer, a, b):
        pl.semaphore_signal(barrier, 1, device_id=device(to_layer, a, b), device_id_type=MESH)

    row_edge = jnp.logical_or(row == 0, row == ROWS - 1)
    col_edge = jnp.logical_or(col == 0, col == COLS - 1)
    rows_beside = jnp.where(row_edge, 1, 2)
    cols_beside = jnp.where(col_edge, 1, 2)
    for a, b in BESIDE:

        @when(beside(a, b))
        def _(a=a, b=b):
            greet(jnp.where(first_layer, 0, layer - 1), a, b)
            greet(jnp.where(last_layer, layer, layer + 1), a, b)

    def greet_layer(k, _):
        greet(lax.rem(layer + k, LAYERS), 0, 0)
        return 0

    lax.fori_loop(1, LAYERS, greet_layer, 0)

    for edge, where in (
        (row == 0, (0, slice(None))),
        (row == ROWS - 1, (TX + 1, slice(None))),
        (col == 0, (slice(None), 0)),
        (col == COLS - 1, (slice(None), TY + 1)),
    ):

        @pl.when(edge)
        def _(where=where):
            def clear(n, _):
                view = framed.at[(n // CHUNKS, lax.rem(n, CHUNKS)) + where]
                view[...] = jnp.zeros(view.shape, jnp.bfloat16)
                return 0

            lax.fori_loop(0, 2 * CHUNKS, clear, 0)

    loading.wait()
    for i in range(TX):
        for j in range(TY):

            def mask(k, _, i=i, j=j):
                present = pattern[i, j, k].astype(jnp.float32).astype(jnp.bfloat16)
                weights[i, j, k] = weights[i, j, k] * present
                return 0

            lax.fori_loop(0, 9, mask, 0)

    partial[...] = jnp.zeros(partial.shape, jnp.float32)
    pl.semaphore_wait(barrier, LAYERS - 1 + ((rows_beside + 1) * (cols_beside + 1) - 1) * 2)

    def own(s, c):
        return (forward_rhs, adjoint_rhs)[s].at[
            :, :, pl.ds(pl.multiple_of(c * CHUNK, CHUNK), CHUNK)
        ]

    def ahead(s, c):
        return pltpu.make_async_remote_copy(
            src_ref=own(s, c),
            dst_ref=coming.at[s, c],
            send_sem=ahead_send.at[s],
            recv_sem=ahead_recv.at[s, c],
            device_id=device(layer - 1 + 2 * s),
            device_id_type=MESH,
        )

    def hop(s, c, a, b, to_layer, source, sem):
        kind = ABOVE if a else ASIDE if b else OWN
        return pltpu.make_async_remote_copy(
            src_ref=source.at[MINE_X[a], MINE_Y[b]],
            dst_ref=framed.at[s, c, THERE_X[a], THERE_Y[b]],
            send_sem=sem,
            recv_sem=recv_sem.at[s, c, kind],
            device_id=device(to_layer, a, b),
            device_id_type=MESH,
        )

    def hops(offsets, s, c, to_layer, source, sem):
        for a, b in offsets:

            @when(beside(a, b))
            def _(a=a, b=b):
                hop(s, c, a, b, to_layer, source, sem).start()

    for s, starts in ((0, first_layer), (1, last_layer)):

        @pl.when(starts)
        def _(s=s):
            def begin(c, _):
                hops(UP + DOWN, s, c, layer, own(s, c), start_send.at[0])
                hops(LEVEL, s, c, layer, own(s, c), start_send.at[1])
                pltpu.make_async_copy(
                    own(s, c), framed.at[s, c, pl.ds(1, TX), pl.ds(1, TY)], recv_sem.at[s, c, OWN]
                ).start()
                return 0

            lax.fori_loop(0, CHUNKS, begin, 0)

    for s, sends in ((0, layer > 0), (1, layer < LAYERS - 1)):

        @pl.when(sends)
        def _(s=s):
            for c in range(CHUNKS):
                ahead(s, c).start()

    kappa_next = coupling[layer_group[jnp.minimum(layer + 1, LAYERS - 1)]]
    kappa_own = coupling[layer_group[layer]]
    late = jnp.where(layer < LAYERS // 2, 0, 1)
    middle = jnp.logical_or(layer == LAYERS // 2 - 1, layer == LAYERS // 2)
    lag = jnp.where(middle, min(LAG, CHUNKS), CHUNKS)

    def await_bytes(view, sem):
        pltpu.make_async_copy(view, view, sem).wait()

    def by_edges(f):
        for on_row_edge in (False, True):
            for on_col_edge in (False, True):

                @pl.when(jnp.logical_and(row_edge == on_row_edge, col_edge == on_col_edge))
                def _(r=1 if on_row_edge else 2, c=1 if on_col_edge else 2):
                    f(r, c)

    def products(s, c, i, j, ks):
        lhs = jnp.concatenate([framed[s, c, i + k // 3, j + k % 3] for k in ks], axis=-1)
        rhs = jnp.concatenate([weights[i, j, k] for k in ks], axis=0)
        return jnp.dot(lhs, rhs, preferred_element_type=jnp.float32)

    inside = {
        (i, j): [
            k for k in range(9) if 0 <= i + k // 3 - 1 < TX and 0 <= j + k % 3 - 1 < TY
        ]
        for i in range(TX)
        for j in range(TY)
    }

    def step(n, _):
        turn = n - lag
        mixed = jnp.logical_and(turn >= 0, n < 2 * CHUNKS - lag)
        phase = jnp.where(turn < 0, 0, jnp.where(mixed, lax.rem(turn, 2), 1))
        c = jnp.where(
            turn < 0, n, jnp.where(mixed, turn // 2 + jnp.where(phase == 0, lag, 0), n - CHUNKS)
        )
        s = lax.rem(phase + late, 2)
        to_layer = layer + 1 - 2 * s
        goes_on = jnp.where(s == 0, layer < LAYERS - 1, layer > 0)
        kappa = jnp.where(s == 0, kappa_next, kappa_own)

        @pl.when(goes_on)
        def _():
            await_bytes(coming.at[s, c], ahead_recv.at[s, c])

        await_bytes(framed.at[s, c, pl.ds(1, TX), pl.ds(1, TY)], recv_sem.at[s, c, OWN])
        sums = {ij: products(s, c, *ij, ks) for ij, ks in inside.items()}

        @by_edges
        def _(rows, cols):
            await_bytes(
                framed.at[s, c, pl.ds(0, rows), pl.ds(0, TY + cols)], recv_sem.at[s, c, ABOVE]
            )
            await_bytes(framed.at[s, c, pl.ds(0, TX), pl.ds(0, cols)], recv_sem.at[s, c, ASIDE])

        for i in range(TX):
            for j in range(TY):
                outside = [k for k in range(9) if k not in inside[i, j]]
                field = (sums[i, j] + products(s, c, i, j, outside)).astype(jnp.bfloat16)
                fields[s, c, i, j] = field
                waves[s, c, i, j] = (
                    coming[s, c, i, j].astype(jnp.float32) + kappa * field.astype(jnp.float32)
                ).astype(jnp.bfloat16)

            @pl.when(goes_on)
            def _(i=i):
                hops(
                    UP if i == 0 else DOWN + LEVEL + [(0, 0)],
                    s,
                    c,
                    to_layer,
                    waves.at[s, c],
                    send_sem.at[s],
                )

        @pl.when(phase == 1)
        def _():
            for i in range(TX):
                for j in range(TY):
                    both = fields[0, c, i, j].astype(jnp.float32) * fields[1, c, i, j].astype(
                        jnp.float32
                    )
                    partial[TY * i + j] += both

        return 0

    lax.fori_loop(0, 2 * CHUNKS, step, 0)

    for t in range(TX * TY):
        mine[pl.ds(t, 1)] = jnp.sum(partial[t], axis=0, keepdims=True) * intersection_scale

    def share(k):
        return pltpu.make_async_remote_copy(
            src_ref=mine,
            dst_ref=theirs.at[k],
            send_sem=sum_send,
            recv_sem=sum_recv,
            device_id=device(lax.rem(layer + k, LAYERS)),
            device_id_type=MESH,
        )

    def start_share(k, _):
        share(k).start()
        return 0

    lax.fori_loop(1, LAYERS, start_share, 0)
    theirs[0] = mine[...]

    for c in range(CHUNKS):
        forward_field[:, :, pl.ds(c * CHUNK, CHUNK)] = fields[0, c]
        adjoint_field[:, :, pl.ds(c * CHUNK, CHUNK)] = fields[1, c]

    for s, starts, stops in ((0, first_layer, last_layer), (1, last_layer, first_layer)):

        @pl.when(jnp.logical_not(starts))
        def _(s=s):
            await_bytes(coming.at[s], ahead_send.at[s])

        @by_edges
        def _(rows, cols, s=s, starts=starts, stops=stops):
            @pl.when(jnp.logical_not(stops))
            def _():
                await_bytes(
                    framed.at[s, :, pl.ds(0, TX + rows), pl.ds(0, TY + cols)], send_sem.at[s]
                )

            @pl.when(starts)
            def _():
                await_bytes(framed.at[s, :, pl.ds(0, rows), pl.ds(0, TY + cols)], start_send.at[0])
                await_bytes(framed.at[s, :, pl.ds(0, TX), pl.ds(0, cols)], start_send.at[1])

    others = theirs.at[pl.ds(1, LAYERS - 1)]
    await_bytes(others, sum_send)
    await_bytes(others, sum_recv)
    for g in range(GROUPS):

        def add(k, total, g=g):
            other = lax.rem(layer - k + LAYERS, LAYERS)
            chosen = jnp.where(layer_group[other] == g, 1.0, 0.0).astype(jnp.float32)
            return total + chosen * theirs[k]

        gradient[g] = lax.fori_loop(0, LAYERS, add, jnp.zeros((TX * TY, TILE), jnp.float32))


def sweeps(forward_rhs, adjoint_rhs, blocks, pattern, coupling, layer_group):
    vmem, smem = (pl.BlockSpec(memory_space=m) for m in (pltpu.VMEM, pltpu.SMEM))
    field = jax.ShapeDtypeStruct((TX, TY, PORTS, TILE), jnp.bfloat16)
    return pl.pallas_call(
        kernel,
        out_shape=(
            field,
            field,
            jax.ShapeDtypeStruct((GROUPS, TX * TY, TILE), jnp.float32),
        ),
        in_specs=[vmem, vmem, pl.BlockSpec(memory_space=pl.ANY), smem, smem, smem],
        out_specs=(vmem, vmem, vmem),
        scratch_shapes=[
            pltpu.VMEM((TX, TY, 9, TILE, TILE), jnp.bfloat16),
            pltpu.VMEM((2, CHUNKS, TX + 2, TY + 2, CHUNK, TILE), jnp.bfloat16),
            pltpu.VMEM((2, CHUNKS, TX, TY, CHUNK, TILE), jnp.bfloat16),
            pltpu.VMEM((2, CHUNKS, TX, TY, CHUNK, TILE), jnp.bfloat16),
            pltpu.VMEM((2, CHUNKS, TX, TY, CHUNK, TILE), jnp.bfloat16),
            pltpu.VMEM((TX * TY, CHUNK, TILE), jnp.float32),
            pltpu.VMEM((TX * TY, TILE), jnp.float32),
            pltpu.VMEM((LAYERS, TX * TY, TILE), jnp.float32),
            pltpu.SemaphoreType.DMA,
            pltpu.SemaphoreType.DMA((2,)),
            pltpu.SemaphoreType.DMA((2, CHUNKS, 3)),
            pltpu.SemaphoreType.DMA((2,)),
            pltpu.SemaphoreType.DMA((2,)),
            pltpu.SemaphoreType.DMA((2, CHUNKS)),
            pltpu.SemaphoreType.DMA,
            pltpu.SemaphoreType.DMA,
        ],
        compiler_params=pltpu.CompilerParams(
            collective_id=0, has_side_effects=True, vmem_limit_bytes=60 << 20
        ),
        name="sweeps",
    )(forward_rhs, adjoint_rhs, blocks, pattern, coupling, layer_group)


def local(sources, adjoint_sources, blocks, pattern, coupling, layer_group, port_cells):
    layer, row, col = (lax.axis_index(a) for a in ("layer", "row", "col"))
    x = row * TX + lax.broadcasted_iota(jnp.int32, (1, TX, TY, TILE), 1)
    y = col * TY + lax.broadcasted_iota(jnp.int32, (1, TX, TY, TILE), 2)
    cell = (x * (COLS * TY) + y) * TILE + lax.broadcasted_iota(jnp.int32, (1, TX, TY, TILE), 3)
    port_map = jnp.where(cell == port_cells[:, None, None, None], port_strength, 0.0)

    def rhs(array, flag):
        whole = array[0].astype(jnp.float32) + jnp.where(flag, 1.0, 0.0) * port_map
        return jnp.transpose(whole.astype(jnp.bfloat16), (1, 2, 0, 3))

    forward_field, adjoint_field, gradient = sweeps(
        rhs(sources, layer == 0),
        rhs(adjoint_sources, layer == LAYERS - 1),
        blocks[0],
        pattern[0],
        coupling,
        layer_group,
    )
    return (
        jnp.transpose(forward_field, (2, 0, 1, 3))[None],
        jnp.transpose(adjoint_field, (2, 0, 1, 3))[None],
        gradient.reshape(GROUPS, TX, TY, TILE),
    )


def solution(mesh):
    placed = (
        P("layer", None, "row", "col", None),
        P("layer", None, "row", "col", None),
        P("layer", "row", "col", None, None, None),
        P("layer", "row", "col", None),
        P(),
        P(),
        P(),
    )
    return jax.shard_map(
        local,
        mesh=mesh,
        in_specs=placed,
        out_specs=(
            P("layer", None, "row", "col", None),
            P("layer", None, "row", "col", None),
            P(None, "row", "col", None),
        ),
        check_vma=False,
    )
```

```python
import functools

import jax
import jax.numpy as jnp
from jax import lax
from jax.experimental import pallas as pl
from jax.experimental.pallas import tpu as pltpu
from jax.sharding import PartitionSpec as P

port_strength = 4.0
intersection_scale = 0.125

LAYERS, ROWS, COLS = 16, 8, 4
TX, TY = 2, 4
PORTS, TILE, GROUPS = 64, 128, 4
CHUNK = 8
CHUNKS = PORTS // CHUNK
LAG = 4
MESH = pl.DeviceIdType.MESH

UP = [(-1, -1), (-1, 1), (-1, 0)]
DOWN = [(1, -1), (1, 1), (1, 0)]
LEVEL = [(0, -1), (0, 1)]
BESIDE = UP + DOWN + LEVEL
MINE_X = {-1: pl.ds(0, 1), 0: pl.ds(0, 2), 1: pl.ds(1, 1)}
MINE_Y = {-1: pl.ds(0, 1), 0: pl.ds(0, 4), 1: pl.ds(3, 1)}
THERE_X = {-1: pl.ds(3, 1), 0: pl.ds(1, 2), 1: pl.ds(0, 1)}
THERE_Y = {-1: pl.ds(5, 1), 0: pl.ds(1, 4), 1: pl.ds(0, 1)}
OWN, ABOVE, ASIDE = 0, 1, 2


def kernel(
    sources,
    adjoint_sources,
    blocks,
    pattern,
    coupling,
    layer_group,
    port_cells,
    forward_field,
    adjoint_field,
    gradient,
    raw,
    ready,
    ported,
    weights,
    framed,
    waves,
    fields,
    coming,
    partial,
    mine,
    theirs,
    load_sem,
    raw_sem,
    out_sem,
    send_sem,
    recv_sem,
    start_send,
    ahead_send,
    ahead_recv,
    sum_send,
    sum_recv,
):
    layer, row, col = (lax.axis_index(a) for a in ("layer", "row", "col"))
    first_layer, last_layer = layer == 0, layer == LAYERS - 1

    loading = pltpu.make_async_copy(blocks, weights, load_sem)
    loading.start()
    late = jnp.where(layer < LAYERS // 2, 0, 1)
    for s in range(2):
        pltpu.make_async_copy((sources, adjoint_sources)[s], raw.at[s], raw_sem.at[s]).start()

    def beside(a, b):
        conds = [[row > 0], [], [row < ROWS - 1]][a + 1] + [[col > 0], [], [col < COLS - 1]][b + 1]
        return functools.reduce(jnp.logical_and, conds) if conds else None

    def when(*conds):
        conds = [c for c in conds if c is not None]
        return pl.when(functools.reduce(jnp.logical_and, conds)) if conds else (lambda f: f())

    def device(to_layer, a=0, b=0):
        return {"layer": to_layer, "row": row + a, "col": col + b}

    barrier = pltpu.get_barrier_semaphore()

    def greet(to_layer, a, b):
        pl.semaphore_signal(barrier, 1, device_id=device(to_layer, a, b), device_id_type=MESH)

    row_edge = jnp.logical_or(row == 0, row == ROWS - 1)
    col_edge = jnp.logical_or(col == 0, col == COLS - 1)
    rows_beside = jnp.where(row_edge, 1, 2)
    cols_beside = jnp.where(col_edge, 1, 2)
    for a, b in BESIDE:

        @when(beside(a, b))
        def _(a=a, b=b):
            greet(jnp.where(first_layer, 0, layer - 1), a, b)
            greet(jnp.where(last_layer, layer, layer + 1), a, b)

    def greet_layer(k, _):
        greet(lax.rem(layer + k, LAYERS), 0, 0)
        return 0

    lax.fori_loop(1, LAYERS, greet_layer, 0)

    for edge, where in (
        (row == 0, (0, slice(None))),
        (row == ROWS - 1, (TX + 1, slice(None))),
        (col == 0, (slice(None), 0)),
        (col == COLS - 1, (slice(None), TY + 1)),
    ):

        @pl.when(edge)
        def _(where=where):
            def clear(n, _):
                view = framed.at[(n // CHUNKS, lax.rem(n, CHUNKS)) + where]
                view[...] = jnp.zeros(view.shape, jnp.bfloat16)
                return 0

            lax.fori_loop(0, 2 * CHUNKS, clear, 0)

    tile = lax.broadcasted_iota(jnp.int32, (TX * TY, TILE), 0)
    cell = (
        (row * TX + tile // TY) * (COLS * TY) + col * TY + lax.rem(tile, TY)
    ) * TILE + lax.broadcasted_iota(jnp.int32, (TX * TY, TILE), 1)

    def prepare(s):
        pltpu.make_async_copy(raw.at[s], raw.at[s], raw_sem.at[s]).wait()
        starts = jnp.where(s == 0, first_layer, last_layer)
        strength = jnp.where(starts, port_strength, 0.0).astype(jnp.float32)

        def one(c, _):
            at = pl.multiple_of(c * CHUNK, CHUNK)
            whole = raw[s, pl.ds(at, CHUNK)].astype(jnp.float32)
            ports = [jnp.where(cell == port_cells[at + p], strength, 0.0) for p in range(CHUNK)]
            by_tile = jnp.swapaxes(whole + jnp.stack(ports), 0, 1).astype(jnp.bfloat16)
            for i in range(TX):
                for j in range(TY):
                    ready[s, c, i, j] = by_tile[TY * i + j]
            return 0

        lax.fori_loop(0, CHUNKS, one, 0)

    prepare(late)
    partial[...] = jnp.zeros(partial.shape, jnp.float32)
    pl.semaphore_wait(barrier, LAYERS - 1 + ((rows_beside + 1) * (cols_beside + 1) - 1) * 2)

    def own(s, c):
        return ready.at[s, c]

    def ahead(s, c):
        return pltpu.make_async_remote_copy(
            src_ref=own(s, c),
            dst_ref=coming.at[s, c],
            send_sem=ahead_send.at[s],
            recv_sem=ahead_recv.at[s, c],
            device_id=device(layer - 1 + 2 * s),
            device_id_type=MESH,
        )

    def hop(s, c, a, b, to_layer, source, sem):
        kind = ABOVE if a else ASIDE if b else OWN
        return pltpu.make_async_remote_copy(
            src_ref=source.at[MINE_X[a], MINE_Y[b]],
            dst_ref=framed.at[s, c, THERE_X[a], THERE_Y[b]],
            send_sem=sem,
            recv_sem=recv_sem.at[s, c, kind],
            device_id=device(to_layer, a, b),
            device_id_type=MESH,
        )

    def hops(offsets, s, c, to_layer, source, sem):
        for a, b in offsets:

            @when(beside(a, b))
            def _(a=a, b=b):
                hop(s, c, a, b, to_layer, source, sem).start()

    for s, starts in ((0, first_layer), (1, last_layer)):

        @pl.when(starts)
        def _(s=s):
            def begin(c, _):
                hops(UP + DOWN, s, c, layer, own(s, c), start_send.at[0])
                hops(LEVEL, s, c, layer, own(s, c), start_send.at[1])
                pltpu.make_async_copy(
                    own(s, c), framed.at[s, c, pl.ds(1, TX), pl.ds(1, TY)], recv_sem.at[s, c, OWN]
                ).start()
                return 0

            lax.fori_loop(0, CHUNKS, begin, 0)

    def send_ahead(s):
        @pl.when(jnp.where(s == 0, layer > 0, layer < LAYERS - 1))
        def _():
            for c in range(CHUNKS):
                ahead(s, c).start()

    send_ahead(late)
    prepare(1 - late)
    send_ahead(1 - late)

    loading.wait()
    for i in range(TX):
        for j in range(TY):

            def mask(k, _, i=i, j=j):
                present = pattern[i, j, k].astype(jnp.float32).astype(jnp.bfloat16)
                weights[i, j, k] = weights[i, j, k] * present
                return 0

            lax.fori_loop(0, 9, mask, 0)

    kappa_next = coupling[layer_group[jnp.minimum(layer + 1, LAYERS - 1)]]
    kappa_own = coupling[layer_group[layer]]
    middle = jnp.logical_or(layer == LAYERS // 2 - 1, layer == LAYERS // 2)
    lag = jnp.where(middle, min(LAG, CHUNKS), CHUNKS)

    def await_bytes(view, sem):
        pltpu.make_async_copy(view, view, sem).wait()

    def by_edges(f):
        for on_row_edge in (False, True):
            for on_col_edge in (False, True):

                @pl.when(jnp.logical_and(row_edge == on_row_edge, col_edge == on_col_edge))
                def _(r=1 if on_row_edge else 2, c=1 if on_col_edge else 2):
                    f(r, c)

    def products(s, c, i, j, ks):
        lhs = jnp.concatenate([framed[s, c, i + k // 3, j + k % 3] for k in ks], axis=-1)
        rhs = jnp.concatenate([weights[i, j, k] for k in ks], axis=0)
        return jnp.dot(lhs, rhs, preferred_element_type=jnp.float32)

    inside = {
        (i, j): [
            k for k in range(9) if 0 <= i + k // 3 - 1 < TX and 0 <= j + k % 3 - 1 < TY
        ]
        for i in range(TX)
        for j in range(TY)
    }

    def step(n, _):
        turn = n - lag
        mixed = jnp.logical_and(turn >= 0, n < 2 * CHUNKS - lag)
        phase = jnp.where(turn < 0, 0, jnp.where(mixed, lax.rem(turn, 2), 1))
        c = jnp.where(
            turn < 0, n, jnp.where(mixed, turn // 2 + jnp.where(phase == 0, lag, 0), n - CHUNKS)
        )
        s = lax.rem(phase + late, 2)
        to_layer = layer + 1 - 2 * s
        goes_on = jnp.where(s == 0, layer < LAYERS - 1, layer > 0)
        kappa = jnp.where(s == 0, kappa_next, kappa_own)

        @pl.when(goes_on)
        def _():
            await_bytes(coming.at[s, c], ahead_recv.at[s, c])

        await_bytes(framed.at[s, c, pl.ds(1, TX), pl.ds(1, TY)], recv_sem.at[s, c, OWN])
        sums = {ij: products(s, c, *ij, ks) for ij, ks in inside.items()}

        @by_edges
        def _(rows, cols):
            await_bytes(
                framed.at[s, c, pl.ds(0, rows), pl.ds(0, TY + cols)], recv_sem.at[s, c, ABOVE]
            )
            await_bytes(framed.at[s, c, pl.ds(0, TX), pl.ds(0, cols)], recv_sem.at[s, c, ASIDE])

        whole = []
        for i in range(TX):
            for j in range(TY):
                outside = [k for k in range(9) if k not in inside[i, j]]
                field = (sums[i, j] + products(s, c, i, j, outside)).astype(jnp.bfloat16)
                fields[s, c, i, j] = field
                whole.append(field.astype(jnp.float32))
                waves[s, c, i, j] = (
                    coming[s, c, i, j].astype(jnp.float32) + kappa * field.astype(jnp.float32)
                ).astype(jnp.bfloat16)

            @pl.when(goes_on)
            def _(i=i):
                hops(
                    UP if i == 0 else DOWN + LEVEL + [(0, 0)],
                    s,
                    c,
                    to_layer,
                    waves.at[s, c],
                    send_sem.at[s],
                )

        ports = pl.ds(pl.multiple_of(c * CHUNK, CHUNK), CHUNK)
        ported[s, ports] = jnp.swapaxes(jnp.stack(whole), 0, 1).astype(jnp.bfloat16)
        for sweep, out in ((0, forward_field), (1, adjoint_field)):

            @pl.when(s == sweep)
            def _(sweep=sweep, out=out):
                pltpu.make_async_copy(
                    ported.at[sweep, ports], out.at[ports], out_sem.at[sweep]
                ).start()

        @pl.when(phase == 1)
        def _():
            for i in range(TX):
                for j in range(TY):
                    both = fields[0, c, i, j].astype(jnp.float32) * fields[1, c, i, j].astype(
                        jnp.float32
                    )
                    partial[TY * i + j] += both

        return 0

    lax.fori_loop(0, 2 * CHUNKS, step, 0)

    for t in range(TX * TY):
        mine[pl.ds(t, 1)] = jnp.sum(partial[t], axis=0, keepdims=True) * intersection_scale

    def share(k):
        return pltpu.make_async_remote_copy(
            src_ref=mine,
            dst_ref=theirs.at[k],
            send_sem=sum_send,
            recv_sem=sum_recv,
            device_id=device(lax.rem(layer + k, LAYERS)),
            device_id_type=MESH,
        )

    def start_share(k, _):
        share(k).start()
        return 0

    lax.fori_loop(1, LAYERS, start_share, 0)
    theirs[0] = mine[...]

    for s, starts, stops in ((0, first_layer, last_layer), (1, last_layer, first_layer)):

        await_bytes(ported.at[s], out_sem.at[s])

        @pl.when(jnp.logical_not(starts))
        def _(s=s):
            await_bytes(coming.at[s], ahead_send.at[s])

        @by_edges
        def _(rows, cols, s=s, starts=starts, stops=stops):
            @pl.when(jnp.logical_not(stops))
            def _():
                await_bytes(
                    framed.at[s, :, pl.ds(0, TX + rows), pl.ds(0, TY + cols)], send_sem.at[s]
                )

            @pl.when(starts)
            def _():
                await_bytes(framed.at[s, :, pl.ds(0, rows), pl.ds(0, TY + cols)], start_send.at[0])
                await_bytes(framed.at[s, :, pl.ds(0, TX), pl.ds(0, cols)], start_send.at[1])

    others = theirs.at[pl.ds(1, LAYERS - 1)]
    await_bytes(others, sum_send)
    await_bytes(others, sum_recv)
    totals = [jnp.zeros((TX * TY, TILE), jnp.float32)] * GROUPS
    for k in range(LAYERS):
        group = layer_group[lax.rem(layer - k + LAYERS, LAYERS)]
        for g in range(GROUPS):
            totals[g] += jnp.where(group == g, 1.0, 0.0).astype(jnp.float32) * theirs[k]
    for g in range(GROUPS):
        gradient[g] = totals[g]


def finish(*refs):
    for a, b in zip(refs[:3], refs[3:]):
        b[...] = a[...]


def sweeps(*arguments):
    vmem, smem, far = (pl.BlockSpec(memory_space=m) for m in (pltpu.VMEM, pltpu.SMEM, pl.ANY))
    field = jax.ShapeDtypeStruct((PORTS, TX * TY, TILE), jnp.bfloat16)
    outputs = (field, field, jax.ShapeDtypeStruct((GROUPS, TX * TY, TILE), jnp.float32))
    results = pl.pallas_call(
        kernel,
        out_shape=outputs,
        in_specs=[far, far, far, smem, smem, smem, smem],
        out_specs=(far, far, vmem),
        scratch_shapes=[
            pltpu.VMEM((2, PORTS, TX * TY, TILE), jnp.bfloat16),
            pltpu.VMEM((2, CHUNKS, TX, TY, CHUNK, TILE), jnp.bfloat16),
            pltpu.VMEM((2, PORTS, TX * TY, TILE), jnp.bfloat16),
            pltpu.VMEM((TX, TY, 9, TILE, TILE), jnp.bfloat16),
            pltpu.VMEM((2, CHUNKS, TX + 2, TY + 2, CHUNK, TILE), jnp.bfloat16),
            pltpu.VMEM((2, CHUNKS, TX, TY, CHUNK, TILE), jnp.bfloat16),
            pltpu.VMEM((2, CHUNKS, TX, TY, CHUNK, TILE), jnp.bfloat16),
            pltpu.VMEM((2, CHUNKS, TX, TY, CHUNK, TILE), jnp.bfloat16),
            pltpu.VMEM((TX * TY, CHUNK, TILE), jnp.float32),
            pltpu.VMEM((TX * TY, TILE), jnp.float32),
            pltpu.VMEM((LAYERS, TX * TY, TILE), jnp.float32),
            pltpu.SemaphoreType.DMA,
            pltpu.SemaphoreType.DMA((2,)),
            pltpu.SemaphoreType.DMA((2,)),
            pltpu.SemaphoreType.DMA((2,)),
            pltpu.SemaphoreType.DMA((2, CHUNKS, 3)),
            pltpu.SemaphoreType.DMA((2,)),
            pltpu.SemaphoreType.DMA((2,)),
            pltpu.SemaphoreType.DMA((2, CHUNKS)),
            pltpu.SemaphoreType.DMA,
            pltpu.SemaphoreType.DMA,
        ],
        compiler_params=pltpu.CompilerParams(
            collective_id=0, has_side_effects=True, vmem_limit_bytes=60 << 20
        ),
        name="sweeps",
    )(*arguments)
    return pl.pallas_call(
        finish,
        out_shape=outputs,
        in_specs=[vmem] * 3,
        out_specs=(vmem,) * 3,
        name="finish",
    )(*results)


def local(sources, adjoint_sources, blocks, pattern, coupling, layer_group, port_cells):
    forward_field, adjoint_field, gradient = sweeps(
        sources.reshape(PORTS, TX * TY, TILE),
        adjoint_sources.reshape(PORTS, TX * TY, TILE),
        blocks[0],
        pattern[0],
        coupling,
        layer_group,
        port_cells,
    )
    return (
        forward_field.reshape(1, PORTS, TX, TY, TILE),
        adjoint_field.reshape(1, PORTS, TX, TY, TILE),
        gradient.reshape(GROUPS, TX, TY, TILE),
    )


def solution(mesh):
    placed = (
        P("layer", None, "row", "col", None),
        P("layer", None, "row", "col", None),
        P("layer", "row", "col", None, None, None),
        P("layer", "row", "col", None),
        P(),
        P(),
        P(),
    )
    return jax.shard_map(
        local,
        mesh=mesh,
        in_specs=placed,
        out_specs=(
            P("layer", None, "row", "col", None),
            P("layer", None, "row", "col", None),
            P(None, "row", "col", None),
        ),
        check_vma=False,
    )
```

```python
import functools

import jax
import jax.numpy as jnp
from jax import lax
from jax.experimental import pallas as pl
from jax.experimental.pallas import tpu as pltpu
from jax.sharding import PartitionSpec as P

port_strength = 4.0
intersection_scale = 0.125

LAYERS, ROWS, COLS = 16, 8, 4
TX, TY = 2, 4
PORTS, TILE, GROUPS = 64, 128, 4
CHUNK = 8
CHUNKS = PORTS // CHUNK
LAG = 4
MESH = pl.DeviceIdType.MESH

UP = [(-1, -1), (-1, 1), (-1, 0)]
DOWN = [(1, -1), (1, 1), (1, 0)]
LEVEL = [(0, -1), (0, 1)]
BESIDE = UP + DOWN + LEVEL
MINE_X = {-1: pl.ds(0, 1), 0: pl.ds(0, 2), 1: pl.ds(1, 1)}
MINE_Y = {-1: pl.ds(0, 1), 0: pl.ds(0, 4), 1: pl.ds(3, 1)}
THERE_X = {-1: pl.ds(3, 1), 0: pl.ds(1, 2), 1: pl.ds(0, 1)}
THERE_Y = {-1: pl.ds(5, 1), 0: pl.ds(1, 4), 1: pl.ds(0, 1)}
OWN, FRAME, ASIDE = 0, 1, 3


def kernel(
    sources,
    adjoint_sources,
    blocks,
    pattern,
    coupling,
    layer_group,
    port_cells,
    forward_field,
    adjoint_field,
    gradient,
    raw,
    ready,
    ported,
    weights,
    framed,
    waves,
    fields,
    coming,
    partial,
    mine,
    theirs,
    load_sem,
    raw_sem,
    out_sem,
    send_sem,
    recv_sem,
    start_send,
    ahead_send,
    ahead_recv,
    sum_send,
    sum_recv,
):
    layer, row, col = (lax.axis_index(a) for a in ("layer", "row", "col"))
    first_layer, last_layer = layer == 0, layer == LAYERS - 1

    loading = pltpu.make_async_copy(blocks, weights, load_sem)
    loading.start()
    late = jnp.where(layer < LAYERS // 2, 0, 1)
    for s in range(2):
        pltpu.make_async_copy((sources, adjoint_sources)[s], raw.at[s], raw_sem.at[s]).start()

    def beside(a, b):
        conds = [[row > 0], [], [row < ROWS - 1]][a + 1] + [[col > 0], [], [col < COLS - 1]][b + 1]
        return functools.reduce(jnp.logical_and, conds) if conds else None

    def when(*conds):
        conds = [c for c in conds if c is not None]
        return pl.when(functools.reduce(jnp.logical_and, conds)) if conds else (lambda f: f())

    def device(to_layer, a=0, b=0):
        return {"layer": to_layer, "row": row + a, "col": col + b}

    barrier = pltpu.get_barrier_semaphore()

    def greet(to_layer, a, b):
        pl.semaphore_signal(barrier, 1, device_id=device(to_layer, a, b), device_id_type=MESH)

    row_edge = jnp.logical_or(row == 0, row == ROWS - 1)
    col_edge = jnp.logical_or(col == 0, col == COLS - 1)
    rows_beside = jnp.where(row_edge, 1, 2)
    cols_beside = jnp.where(col_edge, 1, 2)
    for a, b in BESIDE:

        @when(beside(a, b))
        def _(a=a, b=b):
            greet(jnp.where(first_layer, 0, layer - 1), a, b)
            greet(jnp.where(last_layer, layer, layer + 1), a, b)

    def greet_layer(k, _):
        greet(lax.rem(layer + k, LAYERS), 0, 0)
        return 0

    lax.fori_loop(1, LAYERS, greet_layer, 0)

    for edge, where in (
        (row == 0, (0, slice(None))),
        (row == ROWS - 1, (TX + 1, slice(None))),
        (col == 0, (slice(None), 0)),
        (col == COLS - 1, (slice(None), TY + 1)),
    ):

        @pl.when(edge)
        def _(where=where):
            def clear(n, _):
                view = framed.at[(n // CHUNKS, lax.rem(n, CHUNKS)) + where]
                view[...] = jnp.zeros(view.shape, jnp.bfloat16)
                return 0

            lax.fori_loop(0, 2 * CHUNKS, clear, 0)

    tile = lax.broadcasted_iota(jnp.int32, (TX * TY, TILE), 0)
    cell = (
        (row * TX + tile // TY) * (COLS * TY) + col * TY + lax.rem(tile, TY)
    ) * TILE + lax.broadcasted_iota(jnp.int32, (TX * TY, TILE), 1)

    def prepare(s):
        pltpu.make_async_copy(raw.at[s], raw.at[s], raw_sem.at[s]).wait()
        starts = jnp.where(s == 0, first_layer, last_layer)
        strength = jnp.where(starts, port_strength, 0.0).astype(jnp.float32)

        def one(c, _):
            at = pl.multiple_of(c * CHUNK, CHUNK)
            whole = raw[s, pl.ds(at, CHUNK)].astype(jnp.float32)
            ports = [jnp.where(cell == port_cells[at + p], strength, 0.0) for p in range(CHUNK)]
            by_tile = jnp.swapaxes(whole + jnp.stack(ports), 0, 1).astype(jnp.bfloat16)
            for i in range(TX):
                for j in range(TY):
                    ready[s, c, i, j] = by_tile[TY * i + j]
            return 0

        lax.fori_loop(0, CHUNKS, one, 0)

    prepare(late)
    partial[...] = jnp.zeros(partial.shape, jnp.float32)
    pl.semaphore_wait(barrier, LAYERS - 1 + ((rows_beside + 1) * (cols_beside + 1) - 1) * 2)

    def own(s, c):
        return ready.at[s, c]

    def ahead(s, c):
        return pltpu.make_async_remote_copy(
            src_ref=own(s, c),
            dst_ref=coming.at[s, c],
            send_sem=ahead_send.at[s],
            recv_sem=ahead_recv.at[s, c],
            device_id=device(layer - 1 + 2 * s),
            device_id_type=MESH,
        )

    def hop(s, c, a, b, to_layer, source, sem):
        kind = ASIDE if b else OWN
        return pltpu.make_async_remote_copy(
            src_ref=source.at[MINE_X[a], MINE_Y[b]],
            dst_ref=framed.at[s, c, THERE_X[a], THERE_Y[b]],
            send_sem=sem,
            recv_sem=recv_sem.at[s, c, kind],
            device_id=device(to_layer, a, b),
            device_id_type=MESH,
        )

    def hops(offsets, s, c, to_layer, source, sem):
        for a, b in offsets:

            @when(beside(a, b))
            def _(a=a, b=b):
                hop(s, c, a, b, to_layer, source, sem).start()

    def row_hops(i, s, c, to_layer, source, sem):
        a = 2 * i - 1
        there = jnp.logical_and(row + a >= 0, row + a < ROWS)
        for b in (-1, 1, 0):

            @when(there, beside(0, b))
            def _(b=b):
                pltpu.make_async_remote_copy(
                    src_ref=source.at[pl.ds(i, 1), MINE_Y[b]],
                    dst_ref=framed.at[s, c, pl.ds((TX + 1) * (1 - i), 1), THERE_Y[b]],
                    send_sem=sem,
                    recv_sem=recv_sem.at[s, c, FRAME + i],
                    device_id=device(to_layer, a, b),
                    device_id_type=MESH,
                ).start()

    for s, starts in ((0, first_layer), (1, last_layer)):

        @pl.when(starts)
        def _(s=s):
            def begin(c, _):
                for i in range(TX):
                    row_hops(i, s, c, layer, own(s, c), start_send.at[0])
                hops(LEVEL, s, c, layer, own(s, c), start_send.at[1])
                pltpu.make_async_copy(
                    own(s, c), framed.at[s, c, pl.ds(1, TX), pl.ds(1, TY)], recv_sem.at[s, c, OWN]
                ).start()
                return 0

            lax.fori_loop(0, CHUNKS, begin, 0)

    def send_ahead(s):
        @pl.when(jnp.where(s == 0, layer > 0, layer < LAYERS - 1))
        def _():
            for c in range(CHUNKS):
                ahead(s, c).start()

    send_ahead(late)
    prepare(1 - late)
    send_ahead(1 - late)

    loading.wait()
    for i in range(TX):
        for j in range(TY):

            def mask(k, _, i=i, j=j):
                present = pattern[i, j, k].astype(jnp.float32).astype(jnp.bfloat16)
                weights[i, j, k] = weights[i, j, k] * present
                return 0

            lax.fori_loop(0, 9, mask, 0)

    kappa_next = coupling[layer_group[jnp.minimum(layer + 1, LAYERS - 1)]]
    kappa_own = coupling[layer_group[layer]]
    middle = jnp.logical_or(layer == LAYERS // 2 - 1, layer == LAYERS // 2)
    lag = jnp.where(middle, min(LAG, CHUNKS), CHUNKS)

    def await_bytes(view, sem):
        pltpu.make_async_copy(view, view, sem).wait()

    def by_edges(f):
        for on_row_edge in (False, True):
            for on_col_edge in (False, True):

                @pl.when(jnp.logical_and(row_edge == on_row_edge, col_edge == on_col_edge))
                def _(r=1 if on_row_edge else 2, c=1 if on_col_edge else 2):
                    f(r, c)

    def products(s, c, i, j, terms):
        lhs, rhs = [], []
        for t, b in terms:
            a = (2 * i - 1) * (1 - t)
            lhs.append(framed[s, c, 1 + i + a, 1 + j + b])
            rhs.append(weights[i, j, 3 * (a + 1) + b + 1])
        return jnp.dot(
            jnp.concatenate(lhs, axis=-1),
            jnp.concatenate(rhs, axis=0),
            preferred_element_type=jnp.float32,
        )

    inside = [
        [(t, b) for t in (1, 2) for b in (-1, 0, 1) if 0 <= j + b < TY] for j in range(TY)
    ]
    outside = [
        [(t, b) for t in range(3) for b in (-1, 0, 1) if (t, b) not in inside[j]]
        for j in range(TY)
    ]

    def step(n, _):
        turn = n - lag
        mixed = jnp.logical_and(turn >= 0, n < 2 * CHUNKS - lag)
        phase = jnp.where(turn < 0, 0, jnp.where(mixed, lax.rem(turn, 2), 1))
        c = jnp.where(
            turn < 0, n, jnp.where(mixed, turn // 2 + jnp.where(phase == 0, lag, 0), n - CHUNKS)
        )
        s = lax.rem(phase + late, 2)
        to_layer = layer + 1 - 2 * s
        goes_on = jnp.where(s == 0, layer < LAYERS - 1, layer > 0)
        kappa = jnp.where(s == 0, kappa_next, kappa_own)

        @pl.when(goes_on)
        def _():
            await_bytes(coming.at[s, c], ahead_recv.at[s, c])

        await_bytes(framed.at[s, c, pl.ds(1, TX), pl.ds(1, TY)], recv_sem.at[s, c, OWN])
        first = lax.rem(jnp.where(s == 0, layer, LAYERS - 1 - layer), 2)
        order = (first, 1 - first)
        sums = [[products(s, c, i, j, inside[j]) for j in range(TY)] for i in order]
        for on_edge, cols in ((True, 1), (False, 2)):

            @pl.when(col_edge == on_edge)
            def _(cols=cols):
                await_bytes(
                    framed.at[s, c, pl.ds(0, TX), pl.ds(0, cols)], recv_sem.at[s, c, ASIDE]
                )

        for q, i in enumerate(order):
            framing = jnp.where(i == 0, row > 0, row < ROWS - 1)
            for on_edge, cols in ((True, 1), (False, 2)):

                @pl.when(jnp.logical_and(framing, col_edge == on_edge))
                def _(cols=cols, i=i):
                    await_bytes(
                        framed.at[s, c, pl.ds(0, 1), pl.ds(0, TY + cols)],
                        recv_sem.at[s, c, FRAME + 1 - i],
                    )

            for j in range(TY):
                field = (sums[q][j] + products(s, c, i, j, outside[j])).astype(jnp.bfloat16)
                fields[s, c, i, j] = field
                waves[s, c, i, j] = (
                    coming[s, c, i, j].astype(jnp.float32) + kappa * field.astype(jnp.float32)
                ).astype(jnp.bfloat16)

            @pl.when(goes_on)
            def _(q=q, i=i):
                row_hops(i, s, c, to_layer, waves.at[s, c], send_sem.at[s])
                if q == TX - 1:
                    hops(LEVEL + [(0, 0)], s, c, to_layer, waves.at[s, c], send_sem.at[s])

        whole = [fields[s, c, i, j].astype(jnp.float32) for i in range(TX) for j in range(TY)]
        ports = pl.ds(pl.multiple_of(c * CHUNK, CHUNK), CHUNK)
        ported[s, ports] = jnp.swapaxes(jnp.stack(whole), 0, 1).astype(jnp.bfloat16)
        for sweep, out in ((0, forward_field), (1, adjoint_field)):

            @pl.when(s == sweep)
            def _(sweep=sweep, out=out):
                pltpu.make_async_copy(
                    ported.at[sweep, ports], out.at[ports], out_sem.at[sweep]
                ).start()

        @pl.when(phase == 1)
        def _():
            for i in range(TX):
                for j in range(TY):
                    both = fields[0, c, i, j].astype(jnp.float32) * fields[1, c, i, j].astype(
                        jnp.float32
                    )
                    partial[TY * i + j] += both

        return 0

    lax.fori_loop(0, 2 * CHUNKS, step, 0)

    for t in range(TX * TY):
        mine[pl.ds(t, 1)] = jnp.sum(partial[t], axis=0, keepdims=True) * intersection_scale

    def share(k):
        return pltpu.make_async_remote_copy(
            src_ref=mine,
            dst_ref=theirs.at[k],
            send_sem=sum_send,
            recv_sem=sum_recv,
            device_id=device(lax.rem(layer + k, LAYERS)),
            device_id_type=MESH,
        )

    def start_share(k, _):
        share(k).start()
        return 0

    lax.fori_loop(1, LAYERS, start_share, 0)
    theirs[0] = mine[...]

    for s, starts, stops in ((0, first_layer, last_layer), (1, last_layer, first_layer)):

        await_bytes(ported.at[s], out_sem.at[s])

        @pl.when(jnp.logical_not(starts))
        def _(s=s):
            await_bytes(coming.at[s], ahead_send.at[s])

        @by_edges
        def _(rows, cols, s=s, starts=starts, stops=stops):
            @pl.when(jnp.logical_not(stops))
            def _():
                await_bytes(
                    framed.at[s, :, pl.ds(0, TX + rows), pl.ds(0, TY + cols)], send_sem.at[s]
                )

            @pl.when(starts)
            def _():
                await_bytes(framed.at[s, :, pl.ds(0, rows), pl.ds(0, TY + cols)], start_send.at[0])
                await_bytes(framed.at[s, :, pl.ds(0, TX), pl.ds(0, cols)], start_send.at[1])

    others = theirs.at[pl.ds(1, LAYERS - 1)]
    await_bytes(others, sum_send)
    await_bytes(others, sum_recv)
    totals = [jnp.zeros((TX * TY, TILE), jnp.float32)] * GROUPS
    for k in range(LAYERS):
        group = layer_group[lax.rem(layer - k + LAYERS, LAYERS)]
        for g in range(GROUPS):
            totals[g] += jnp.where(group == g, 1.0, 0.0).astype(jnp.float32) * theirs[k]
    for g in range(GROUPS):
        gradient[g] = totals[g]


def finish(*refs):
    for a, b in zip(refs[:3], refs[3:]):
        b[...] = a[...]


def sweeps(*arguments):
    vmem, smem, far = (pl.BlockSpec(memory_space=m) for m in (pltpu.VMEM, pltpu.SMEM, pl.ANY))
    field = jax.ShapeDtypeStruct((PORTS, TX * TY, TILE), jnp.bfloat16)
    outputs = (field, field, jax.ShapeDtypeStruct((GROUPS, TX * TY, TILE), jnp.float32))
    results = pl.pallas_call(
        kernel,
        out_shape=outputs,
        in_specs=[far, far, far, smem, smem, smem, smem],
        out_specs=(far, far, vmem),
        scratch_shapes=[
            pltpu.VMEM((2, PORTS, TX * TY, TILE), jnp.bfloat16),
            pltpu.VMEM((2, CHUNKS, TX, TY, CHUNK, TILE), jnp.bfloat16),
            pltpu.VMEM((2, PORTS, TX * TY, TILE), jnp.bfloat16),
            pltpu.VMEM((TX, TY, 9, TILE, TILE), jnp.bfloat16),
            pltpu.VMEM((2, CHUNKS, TX + 2, TY + 2, CHUNK, TILE), jnp.bfloat16),
            pltpu.VMEM((2, CHUNKS, TX, TY, CHUNK, TILE), jnp.bfloat16),
            pltpu.VMEM((2, CHUNKS, TX, TY, CHUNK, TILE), jnp.bfloat16),
            pltpu.VMEM((2, CHUNKS, TX, TY, CHUNK, TILE), jnp.bfloat16),
            pltpu.VMEM((TX * TY, CHUNK, TILE), jnp.float32),
            pltpu.VMEM((TX * TY, TILE), jnp.float32),
            pltpu.VMEM((LAYERS, TX * TY, TILE), jnp.float32),
            pltpu.SemaphoreType.DMA,
            pltpu.SemaphoreType.DMA((2,)),
            pltpu.SemaphoreType.DMA((2,)),
            pltpu.SemaphoreType.DMA((2,)),
            pltpu.SemaphoreType.DMA((2, CHUNKS, 4)),
            pltpu.SemaphoreType.DMA((2,)),
            pltpu.SemaphoreType.DMA((2,)),
            pltpu.SemaphoreType.DMA((2, CHUNKS)),
            pltpu.SemaphoreType.DMA,
            pltpu.SemaphoreType.DMA,
        ],
        compiler_params=pltpu.CompilerParams(
            collective_id=0, has_side_effects=True, vmem_limit_bytes=60 << 20
        ),
        name="sweeps",
    )(*arguments)
    return pl.pallas_call(
        finish,
        out_shape=outputs,
        in_specs=[vmem] * 3,
        out_specs=(vmem,) * 3,
        name="finish",
    )(*results)


def local(sources, adjoint_sources, blocks, pattern, coupling, layer_group, port_cells):
    forward_field, adjoint_field, gradient = sweeps(
        sources.reshape(PORTS, TX * TY, TILE),
        adjoint_sources.reshape(PORTS, TX * TY, TILE),
        blocks[0],
        pattern[0],
        coupling,
        layer_group,
        port_cells,
    )
    return (
        forward_field.reshape(1, PORTS, TX, TY, TILE),
        adjoint_field.reshape(1, PORTS, TX, TY, TILE),
        gradient.reshape(GROUPS, TX, TY, TILE),
    )


def solution(mesh):
    placed = (
        P("layer", None, "row", "col", None),
        P("layer", None, "row", "col", None),
        P("layer", "row", "col", None, None, None),
        P("layer", "row", "col", None),
        P(),
        P(),
        P(),
    )
    return jax.shard_map(
        local,
        mesh=mesh,
        in_specs=placed,
        out_specs=(
            P("layer", None, "row", "col", None),
            P("layer", None, "row", "col", None),
            P(None, "row", "col", None),
        ),
        check_vma=False,
    )
```

```python
import functools

import jax
import jax.numpy as jnp
from jax import lax
from jax.experimental import pallas as pl
from jax.experimental.pallas import tpu as pltpu
from jax.sharding import PartitionSpec as P

port_strength = 4.0
intersection_scale = 0.125

LAYERS, ROWS, COLS = 16, 8, 4
TX, TY = 2, 4
PORTS, TILE, GROUPS = 64, 128, 4
CHUNK = 8
CHUNKS = PORTS // CHUNK
LAG = 4
MESH = pl.DeviceIdType.MESH

UP = [(-1, -1), (-1, 1), (-1, 0)]
DOWN = [(1, -1), (1, 1), (1, 0)]
LEVEL = [(0, -1), (0, 1)]
BESIDE = UP + DOWN + LEVEL
MINE_X = {-1: pl.ds(0, 1), 0: pl.ds(0, 2), 1: pl.ds(1, 1)}
MINE_Y = {-1: pl.ds(0, 1), 0: pl.ds(0, 4), 1: pl.ds(3, 1)}
THERE_X = {-1: pl.ds(3, 1), 0: pl.ds(1, 2), 1: pl.ds(0, 1)}
THERE_Y = {-1: pl.ds(5, 1), 0: pl.ds(1, 4), 1: pl.ds(0, 1)}
OWN, FRAME, ASIDE = 0, 1, 3


def kernel(
    sources,
    adjoint_sources,
    blocks,
    pattern,
    coupling,
    layer_group,
    port_cells,
    forward_field,
    adjoint_field,
    gradient,
    raw,
    ready,
    ported,
    weights,
    framed,
    waves,
    fields,
    coming,
    partial,
    mine,
    theirs,
    load_sem,
    raw_sem,
    out_sem,
    send_sem,
    recv_sem,
    start_send,
    ahead_send,
    ahead_recv,
    sum_send,
    sum_recv,
):
    layer, row, col = (lax.axis_index(a) for a in ("layer", "row", "col"))
    first_layer, last_layer = layer == 0, layer == LAYERS - 1

    loading = pltpu.make_async_copy(blocks, weights, load_sem)
    loading.start()
    late = jnp.where(layer < LAYERS // 2, 0, 1)
    for s in range(2):
        pltpu.make_async_copy((sources, adjoint_sources)[s], raw.at[s], raw_sem.at[s]).start()

    def beside(a, b):
        conds = [[row > 0], [], [row < ROWS - 1]][a + 1] + [[col > 0], [], [col < COLS - 1]][b + 1]
        return functools.reduce(jnp.logical_and, conds) if conds else None

    def when(*conds):
        conds = [c for c in conds if c is not None]
        return pl.when(functools.reduce(jnp.logical_and, conds)) if conds else (lambda f: f())

    def device(to_layer, a=0, b=0):
        return {"layer": to_layer, "row": row + a, "col": col + b}

    barrier = pltpu.get_barrier_semaphore()

    def greet(to_layer, a, b):
        pl.semaphore_signal(barrier, 1, device_id=device(to_layer, a, b), device_id_type=MESH)

    row_edge = jnp.logical_or(row == 0, row == ROWS - 1)
    col_edge = jnp.logical_or(col == 0, col == COLS - 1)
    rows_beside = jnp.where(row_edge, 1, 2)
    cols_beside = jnp.where(col_edge, 1, 2)
    for a, b in BESIDE:

        @when(beside(a, b))
        def _(a=a, b=b):
            greet(jnp.where(first_layer, 0, layer - 1), a, b)
            greet(jnp.where(last_layer, layer, layer + 1), a, b)

    def greet_layer(k, _):
        greet(lax.rem(layer + k, LAYERS), 0, 0)
        return 0

    lax.fori_loop(1, LAYERS, greet_layer, 0)

    for edge, where in (
        (row == 0, (0, slice(None))),
        (row == ROWS - 1, (TX + 1, slice(None))),
        (col == 0, (slice(None), 0)),
        (col == COLS - 1, (slice(None), TY + 1)),
    ):

        @pl.when(edge)
        def _(where=where):
            def clear(n, _):
                view = framed.at[(n // CHUNKS, lax.rem(n, CHUNKS)) + where]
                view[...] = jnp.zeros(view.shape, jnp.bfloat16)
                return 0

            lax.fori_loop(0, 2 * CHUNKS, clear, 0)

    tile = lax.broadcasted_iota(jnp.int32, (TX * TY, TILE), 0)
    cell = (
        (row * TX + tile // TY) * (COLS * TY) + col * TY + lax.rem(tile, TY)
    ) * TILE + lax.broadcasted_iota(jnp.int32, (TX * TY, TILE), 1)

    def prepare(s):
        pltpu.make_async_copy(raw.at[s], raw.at[s], raw_sem.at[s]).wait()
        starts = jnp.where(s == 0, first_layer, last_layer)
        strength = jnp.where(starts, port_strength, 0.0).astype(jnp.float32)

        def one(c, _):
            at = pl.multiple_of(c * CHUNK, CHUNK)
            whole = raw[s, pl.ds(at, CHUNK)].astype(jnp.float32)
            ports = [jnp.where(cell == port_cells[at + p], strength, 0.0) for p in range(CHUNK)]
            by_tile = jnp.swapaxes(whole + jnp.stack(ports), 0, 1).astype(jnp.bfloat16)
            for i in range(TX):
                for j in range(TY):
                    ready[s, c, i, j] = by_tile[TY * i + j]
            return 0

        lax.fori_loop(0, CHUNKS, one, 0)

    prepare(late)
    partial[...] = jnp.zeros(partial.shape, jnp.float32)
    pl.semaphore_wait(barrier, LAYERS - 1 + ((rows_beside + 1) * (cols_beside + 1) - 1) * 2)

    def own(s, c):
        return ready.at[s, c]

    def ahead(s, c):
        return pltpu.make_async_remote_copy(
            src_ref=own(s, c),
            dst_ref=coming.at[s, c],
            send_sem=ahead_send.at[s],
            recv_sem=ahead_recv.at[s, c],
            device_id=device(layer - 1 + 2 * s),
            device_id_type=MESH,
        )

    def hop(s, c, a, b, to_layer, source, sem):
        kind = ASIDE if b else OWN
        return pltpu.make_async_remote_copy(
            src_ref=source.at[MINE_X[a], MINE_Y[b]],
            dst_ref=framed.at[s, c, THERE_X[a], THERE_Y[b]],
            send_sem=sem,
            recv_sem=recv_sem.at[s, c, kind],
            device_id=device(to_layer, a, b),
            device_id_type=MESH,
        )

    def hops(offsets, s, c, to_layer, source, sem):
        for a, b in offsets:

            @when(beside(a, b))
            def _(a=a, b=b):
                hop(s, c, a, b, to_layer, source, sem).start()

    def row_hops(i, s, c, to_layer, source, sem):
        a = 2 * i - 1
        there = jnp.logical_and(row + a >= 0, row + a < ROWS)
        for b in (-1, 1, 0):

            @when(there, beside(0, b))
            def _(b=b):
                pltpu.make_async_remote_copy(
                    src_ref=source.at[pl.ds(i, 1), MINE_Y[b]],
                    dst_ref=framed.at[s, c, pl.ds((TX + 1) * (1 - i), 1), THERE_Y[b]],
                    send_sem=sem,
                    recv_sem=recv_sem.at[s, c, FRAME + i],
                    device_id=device(to_layer, a, b),
                    device_id_type=MESH,
                ).start()

    for s, starts in ((0, first_layer), (1, last_layer)):

        @pl.when(starts)
        def _(s=s):
            def begin(c, _):
                for i in range(TX):
                    row_hops(i, s, c, layer, own(s, c), start_send.at[0])
                hops(LEVEL, s, c, layer, own(s, c), start_send.at[1])
                pltpu.make_async_copy(
                    own(s, c), framed.at[s, c, pl.ds(1, TX), pl.ds(1, TY)], recv_sem.at[s, c, OWN]
                ).start()
                return 0

            lax.fori_loop(0, CHUNKS, begin, 0)

    def send_ahead(s):
        @pl.when(jnp.where(s == 0, layer > 0, layer < LAYERS - 1))
        def _():
            for c in range(CHUNKS):
                ahead(s, c).start()

    send_ahead(late)
    prepare(1 - late)
    send_ahead(1 - late)

    loading.wait()
    for i in range(TX):
        for j in range(TY):

            def mask(k, _, i=i, j=j):
                present = pattern[i, j, k].astype(jnp.float32).astype(jnp.bfloat16)
                weights[i, j, k] = weights[i, j, k] * present
                return 0

            lax.fori_loop(0, 9, mask, 0)

    kappa_next = coupling[layer_group[jnp.minimum(layer + 1, LAYERS - 1)]]
    kappa_own = coupling[layer_group[layer]]
    middle = jnp.logical_or(layer == LAYERS // 2 - 1, layer == LAYERS // 2)
    lag = jnp.where(middle, min(LAG, CHUNKS), CHUNKS)

    def await_bytes(view, sem):
        pltpu.make_async_copy(view, view, sem).wait()

    def by_edges(f):
        for on_row_edge in (False, True):
            for on_col_edge in (False, True):

                @pl.when(jnp.logical_and(row_edge == on_row_edge, col_edge == on_col_edge))
                def _(r=1 if on_row_edge else 2, c=1 if on_col_edge else 2):
                    f(r, c)

    def products(s, c, i, j, terms):
        lhs, rhs = [], []
        for t, b in terms:
            a = (2 * i - 1) * (1 - t)
            lhs.append(framed[s, c, 1 + i + a, 1 + j + b])
            rhs.append(weights[i, j, 3 * (a + 1) + b + 1])
        return jnp.dot(
            jnp.concatenate(lhs, axis=-1),
            jnp.concatenate(rhs, axis=0),
            preferred_element_type=jnp.float32,
        )

    inside = [
        [(t, b) for t in (1, 2) for b in (-1, 0, 1) if 0 <= j + b < TY] for j in range(TY)
    ]
    outside = [
        [(t, b) for t in range(3) for b in (-1, 0, 1) if (t, b) not in inside[j]]
        for j in range(TY)
    ]

    def step(n, _):
        turn = n - lag
        mixed = jnp.logical_and(turn >= 0, n < 2 * CHUNKS - lag)
        phase = jnp.where(turn < 0, 0, jnp.where(mixed, lax.rem(turn, 2), 1))
        c = jnp.where(
            turn < 0, n, jnp.where(mixed, turn // 2 + jnp.where(phase == 0, lag, 0), n - CHUNKS)
        )
        s = lax.rem(phase + late, 2)
        to_layer = layer + 1 - 2 * s
        goes_on = jnp.where(s == 0, layer < LAYERS - 1, layer > 0)
        kappa = jnp.where(s == 0, kappa_next, kappa_own)

        @pl.when(goes_on)
        def _():
            await_bytes(coming.at[s, c], ahead_recv.at[s, c])

        await_bytes(framed.at[s, c, pl.ds(1, TX), pl.ds(1, TY)], recv_sem.at[s, c, OWN])
        first = lax.rem(jnp.where(s == 0, layer, LAYERS - 1 - layer), 2)
        order = (first, 1 - first)
        sums = [[products(s, c, i, j, inside[j]) for j in range(TY)] for i in order]
        for on_edge, cols in ((True, 1), (False, 2)):

            @pl.when(col_edge == on_edge)
            def _(cols=cols):
                await_bytes(
                    framed.at[s, c, pl.ds(0, TX), pl.ds(0, cols)], recv_sem.at[s, c, ASIDE]
                )

        for q, i in enumerate(order):
            framing = jnp.where(i == 0, row > 0, row < ROWS - 1)
            for on_edge, cols in ((True, 1), (False, 2)):

                @pl.when(jnp.logical_and(framing, col_edge == on_edge))
                def _(cols=cols, i=i):
                    await_bytes(
                        framed.at[s, c, pl.ds(0, 1), pl.ds(0, TY + cols)],
                        recv_sem.at[s, c, FRAME + 1 - i],
                    )

            for j in range(TY):
                field = (sums[q][j] + products(s, c, i, j, outside[j])).astype(jnp.bfloat16)
                fields[s, c, i, j] = field
                waves[s, c, i, j] = (
                    coming[s, c, i, j].astype(jnp.float32) + kappa * field.astype(jnp.float32)
                ).astype(jnp.bfloat16)

            @pl.when(goes_on)
            def _(q=q, i=i):
                row_hops(i, s, c, to_layer, waves.at[s, c], send_sem.at[s])
                if q == TX - 1:
                    hops(LEVEL, s, c, to_layer, waves.at[s, c], send_sem.at[s])
                pltpu.make_async_remote_copy(
                    src_ref=waves.at[s, c, pl.ds(i, 1)],
                    dst_ref=framed.at[s, c, pl.ds(1 + i, 1), pl.ds(1, TY)],
                    send_sem=send_sem.at[s],
                    recv_sem=recv_sem.at[s, c, OWN],
                    device_id=device(to_layer),
                    device_id_type=MESH,
                ).start()

        whole = [fields[s, c, i, j].astype(jnp.float32) for i in range(TX) for j in range(TY)]
        ports = pl.ds(pl.multiple_of(c * CHUNK, CHUNK), CHUNK)
        ported[s, ports] = jnp.swapaxes(jnp.stack(whole), 0, 1).astype(jnp.bfloat16)
        for sweep, out in ((0, forward_field), (1, adjoint_field)):

            @pl.when(s == sweep)
            def _(sweep=sweep, out=out):
                pltpu.make_async_copy(
                    ported.at[sweep, ports], out.at[ports], out_sem.at[sweep]
                ).start()

        @pl.when(phase == 1)
        def _():
            for i in range(TX):
                for j in range(TY):
                    both = fields[0, c, i, j].astype(jnp.float32) * fields[1, c, i, j].astype(
                        jnp.float32
                    )
                    partial[TY * i + j] += both

        return 0

    lax.fori_loop(0, 2 * CHUNKS, step, 0)

    for t in range(TX * TY):
        mine[pl.ds(t, 1)] = jnp.sum(partial[t], axis=0, keepdims=True) * intersection_scale

    def share(k):
        return pltpu.make_async_remote_copy(
            src_ref=mine,
            dst_ref=theirs.at[k],
            send_sem=sum_send,
            recv_sem=sum_recv,
            device_id=device(lax.rem(layer + k, LAYERS)),
            device_id_type=MESH,
        )

    def start_share(k, _):
        share(k).start()
        return 0

    lax.fori_loop(1, LAYERS, start_share, 0)
    theirs[0] = mine[...]

    for s, starts, stops in ((0, first_layer, last_layer), (1, last_layer, first_layer)):

        await_bytes(ported.at[s], out_sem.at[s])

        @pl.when(jnp.logical_not(starts))
        def _(s=s):
            await_bytes(coming.at[s], ahead_send.at[s])

        @by_edges
        def _(rows, cols, s=s, starts=starts, stops=stops):
            @pl.when(jnp.logical_not(stops))
            def _():
                await_bytes(
                    framed.at[s, :, pl.ds(0, TX + rows), pl.ds(0, TY + cols)], send_sem.at[s]
                )

            @pl.when(starts)
            def _():
                await_bytes(framed.at[s, :, pl.ds(0, rows), pl.ds(0, TY + cols)], start_send.at[0])
                await_bytes(framed.at[s, :, pl.ds(0, TX), pl.ds(0, cols)], start_send.at[1])

    others = theirs.at[pl.ds(1, LAYERS - 1)]
    await_bytes(others, sum_send)
    await_bytes(others, sum_recv)
    totals = [jnp.zeros((TX * TY, TILE), jnp.float32)] * GROUPS
    for k in range(LAYERS):
        group = layer_group[lax.rem(layer - k + LAYERS, LAYERS)]
        for g in range(GROUPS):
            totals[g] += jnp.where(group == g, 1.0, 0.0).astype(jnp.float32) * theirs[k]
    for g in range(GROUPS):
        gradient[g] = totals[g]


def finish(*refs):
    for a, b in zip(refs[:3], refs[3:]):
        b[...] = a[...]


def sweeps(*arguments):
    vmem, smem, far = (pl.BlockSpec(memory_space=m) for m in (pltpu.VMEM, pltpu.SMEM, pl.ANY))
    field = jax.ShapeDtypeStruct((PORTS, TX * TY, TILE), jnp.bfloat16)
    outputs = (field, field, jax.ShapeDtypeStruct((GROUPS, TX * TY, TILE), jnp.float32))
    results = pl.pallas_call(
        kernel,
        out_shape=outputs,
        in_specs=[far, far, far, smem, smem, smem, smem],
        out_specs=(far, far, vmem),
        scratch_shapes=[
            pltpu.VMEM((2, PORTS, TX * TY, TILE), jnp.bfloat16),
            pltpu.VMEM((2, CHUNKS, TX, TY, CHUNK, TILE), jnp.bfloat16),
            pltpu.VMEM((2, PORTS, TX * TY, TILE), jnp.bfloat16),
            pltpu.VMEM((TX, TY, 9, TILE, TILE), jnp.bfloat16),
            pltpu.VMEM((2, CHUNKS, TX + 2, TY + 2, CHUNK, TILE), jnp.bfloat16),
            pltpu.VMEM((2, CHUNKS, TX, TY, CHUNK, TILE), jnp.bfloat16),
            pltpu.VMEM((2, CHUNKS, TX, TY, CHUNK, TILE), jnp.bfloat16),
            pltpu.VMEM((2, CHUNKS, TX, TY, CHUNK, TILE), jnp.bfloat16),
            pltpu.VMEM((TX * TY, CHUNK, TILE), jnp.float32),
            pltpu.VMEM((TX * TY, TILE), jnp.float32),
            pltpu.VMEM((LAYERS, TX * TY, TILE), jnp.float32),
            pltpu.SemaphoreType.DMA,
            pltpu.SemaphoreType.DMA((2,)),
            pltpu.SemaphoreType.DMA((2,)),
            pltpu.SemaphoreType.DMA((2,)),
            pltpu.SemaphoreType.DMA((2, CHUNKS, 4)),
            pltpu.SemaphoreType.DMA((2,)),
            pltpu.SemaphoreType.DMA((2,)),
            pltpu.SemaphoreType.DMA((2, CHUNKS)),
            pltpu.SemaphoreType.DMA,
            pltpu.SemaphoreType.DMA,
        ],
        compiler_params=pltpu.CompilerParams(
            collective_id=0, has_side_effects=True, vmem_limit_bytes=60 << 20
        ),
        name="sweeps",
    )(*arguments)
    return pl.pallas_call(
        finish,
        out_shape=outputs,
        in_specs=[vmem] * 3,
        out_specs=(vmem,) * 3,
        name="finish",
    )(*results)


def local(sources, adjoint_sources, blocks, pattern, coupling, layer_group, port_cells):
    forward_field, adjoint_field, gradient = sweeps(
        sources.reshape(PORTS, TX * TY, TILE),
        adjoint_sources.reshape(PORTS, TX * TY, TILE),
        blocks[0],
        pattern[0],
        coupling,
        layer_group,
        port_cells,
    )
    return (
        forward_field.reshape(1, PORTS, TX, TY, TILE),
        adjoint_field.reshape(1, PORTS, TX, TY, TILE),
        gradient.reshape(GROUPS, TX, TY, TILE),
    )


def solution(mesh):
    placed = (
        P("layer", None, "row", "col", None),
        P("layer", None, "row", "col", None),
        P("layer", "row", "col", None, None, None),
        P("layer", "row", "col", None),
        P(),
        P(),
        P(),
    )
    return jax.shard_map(
        local,
        mesh=mesh,
        in_specs=placed,
        out_specs=(
            P("layer", None, "row", "col", None),
            P("layer", None, "row", "col", None),
            P(None, "row", "col", None),
        ),
        check_vma=False,
    )
```
